32 devices in a mesh: row: 8 (over z, y), col: 4 (over x, core).
Axes of the slice: x: 2, y: 2, z: 4, core: 2. Of those that a mesh axis runs over, the one named last changes fastest.
Arguments:
- matrix: bfloat16 [6, 4096, 12, 2048], P(None, 'row', None, 'col'), may hold values from -6 to 6
- multiplier: bfloat16 [2, 512, 512], replicated
- checksum_weight: float32 [6, 4096], P(None, 'row')
Outputs:
- factored: bfloat16 [6, 4096, 12, 2048], P(None, 'row', None, 'col')
- group_checksum: float32 [8, 12, 2048], P('row', None, 'col')
- total_checksum: float32 [12, 2048], P(None, 'col')
The draws below stay inside these ranges and needn't reach their ends.
All inputs are finite; a program needn't handle non-finite values.
Results may differ from the reference program's by a relative error of at most 0.0056.
Values may be sent and summed in bfloat16 or wider, within the bound.
A program may use at most 256 MiB of HBM per device.

```python
import math
import jax
import jax.numpy as jnp
from jax import lax

PANEL_WIDTH = 512
ORDER = 24576
ELIMINATION_STEPS = 2
RBD = 6
CBD = 12
N_ROW = 8
N_COL = 4


def draw_multiplier(key, part):
    first_key, second_key = jax.random.split(jax.random.fold_in(key, 11))
    base = 2.0 * math.sqrt(PANEL_WIDTH)
    diagonal = jnp.exp(jax.random.uniform(first_key, (ELIMINATION_STEPS, PANEL_WIDTH), jnp.float32, math.log(0.5), math.log(2.0))) / base
    offdiag = jax.random.normal(second_key, (ELIMINATION_STEPS, PANEL_WIDTH, PANEL_WIDTH), jnp.float32) * (0.3 / (base * math.sqrt(PANEL_WIDTH)))
    identity = jnp.eye(PANEL_WIDTH, dtype=jnp.float32)
    return (offdiag + identity[None, :, :] * diagonal[:, :, None]).astype(jnp.bfloat16)


def draw_checksum_weight(key, part):
    sub_key = jax.random.fold_in(key, 23)
    group = (jnp.arange(N_ROW * PANEL_WIDTH, dtype=jnp.int32) // PANEL_WIDTH).astype(jnp.float32)
    rising = 1.0 + 2.0 * group / max(N_ROW - 1, 1)
    scale = 0.5 / math.sqrt(RBD * PANEL_WIDTH)
    values = jax.random.normal(sub_key, (RBD, N_ROW * PANEL_WIDTH), jnp.float32)
    return (values * rising[None, :] * scale).astype(jnp.float32)


def level_of(key, shape, shards, least, high):
    factor_of, own = 1.0, jax.random.fold_in(key, 6)
    for dim, parts in shards:
        draws = jnp.exp(jax.random.uniform(jax.random.fold_in(own, dim), (parts,), jnp.float32, least / len(shards), high / len(shards)))
        factor_of = factor_of * jnp.repeat(draws, shape[dim] // parts).reshape([-1 if axis == dim else 1 for axis in range(len(shape))])
    return factor_of


def gaussian(key, shape, spread, reach, shards=(), kind=jnp.bfloat16):
    values = jax.random.normal(key, shape, jnp.float32) * spread
    if len(shards) > 0:
        values = level_of(key, shape, shards, -0.22, 0.18) * values
    return jnp.clip(values, min=-reach, max=reach).astype(kind)


def setup_inputs(seed: int = 0) -> dict:
    splits = jax.random.split(jax.random.key(seed), 4)
    return {
        "matrix": gaussian(splits[0], (RBD, N_ROW * PANEL_WIDTH, CBD, N_COL * PANEL_WIDTH), 1.0, 6.0, ((1, 8), (3, 4))),
        "multiplier": draw_multiplier(jax.random.fold_in(splits[3], 71), 0),
        "checksum_weight": draw_checksum_weight(jax.random.fold_in(splits[3], 71), 0),
    }


slab_rows = 4096


def reference(matrix, multiplier, checksum_weight):
    highest_precision = lax.Precision.HIGHEST
    full_matrix_input = matrix.reshape(ORDER, ORDER)
    weight_rows = checksum_weight.reshape(ORDER)
    group_of_row = (jnp.arange(ORDER, dtype=jnp.int32) // PANEL_WIDTH) % N_ROW
    selector = (group_of_row[None, :] == jnp.arange(N_ROW, dtype=jnp.int32)[:, None]).astype(jnp.float32) * weight_rows[None, :]
    checks = jnp.dot(selector, full_matrix_input.astype(jnp.float32), precision=highest_precision, preferred_element_type=jnp.float32)
    column_ids = jnp.arange(ORDER, dtype=jnp.int32)
    for eliminate_block in range(ELIMINATION_STEPS):
        column_begin = eliminate_block * PANEL_WIDTH
        column_end = column_begin + PANEL_WIDTH
        lower_triangle = jnp.dot(full_matrix_input[column_end:, column_begin:column_end].astype(jnp.float32), multiplier[eliminate_block].astype(jnp.float32), precision=highest_precision, preferred_element_type=jnp.float32).astype(jnp.bfloat16)
        pivot_row_band = jnp.where(column_ids[None, :] >= column_end, full_matrix_input[column_begin:column_end, :].astype(jnp.float32), jnp.float32(0.0))
        summed = jnp.dot(selector[:, column_end:], lower_triangle.astype(jnp.float32), precision=highest_precision, preferred_element_type=jnp.float32)
        checks = checks - jnp.dot(summed, pivot_row_band, precision=highest_precision, preferred_element_type=jnp.float32)
        lower_f = lower_triangle.astype(jnp.float32)
        pieces = [full_matrix_input[:column_end]]
        for slab_start in range(column_end, ORDER, slab_rows):
            slab_stop = min(slab_start + slab_rows, ORDER)
            product = jnp.dot(lower_f[slab_start - column_end:slab_stop - column_end], pivot_row_band, precision=highest_precision, preferred_element_type=jnp.float32)
            pieces.append((full_matrix_input[slab_start:slab_stop].astype(jnp.float32) - product).astype(jnp.bfloat16))
        full_matrix_input = jnp.concatenate(pieces, axis=0)
        full_matrix_input = full_matrix_input.at[column_end:, column_begin:column_end].set(lower_triangle)
    factored = full_matrix_input.reshape(RBD, N_ROW * PANEL_WIDTH, CBD, N_COL * PANEL_WIDTH)
    return factored, checks.reshape(N_ROW, CBD, N_COL * PANEL_WIDTH), jnp.sum(checks, axis=0).reshape(CBD, N_COL * PANEL_WIDTH)
```

```python
import functools

import jax
import jax.numpy as jnp
from jax import lax
from jax.experimental import pallas as pl
from jax.experimental.pallas import tpu as pltpu
from jax.sharding import PartitionSpec as P

SUBS = 4
MESH = pl.DeviceIdType.MESH


def kernel(dims, mt, mult, g, out, group, total, ubuf, lraw, lcat, ebuf, lzb, ucat, min_, mout,
           gcol, csum, crow, cbuf, usem, uzs, uys, lsem, lxs, lks, esem, ezs, eys, eks,
           insem, outsem, csend, crecv):
    grid_rows, grid_cols, row_blocks, col_blocks, size = dims
    f32, bf16 = jnp.float32, jnp.bfloat16
    sub, half = size // SUBS, size // 2
    me_r, me_c = lax.axis_index("row"), lax.axis_index("col")
    z, y, x, k = me_r // 2, me_r % 2, me_c // 2, me_c % 2
    depth_z, depth_x = grid_rows // 2, grid_cols // 2
    up, across = me_r + 2, me_r + 1 - 2 * y
    beyond, sibling = me_c + 2, me_c + 1 - 2 * k
    n_sub, n_unit = SUBS * col_blocks, 2 * col_blocks

    def remote(ref, send, recv, axis, to):
        return pltpu.make_async_remote_copy(
            src_ref=ref, dst_ref=ref, send_sem=send, recv_sem=recv,
            device_id={axis: to}, device_id_type=MESH)

    def u_rows(t):
        return pl.ds(pl.multiple_of((t % SUBS) * sub, sub), sub)

    def u_ref(band, t):
        return ubuf.at[band, t // SUBS, u_rows(t), :]

    def u_load(t):
        return pltpu.make_async_copy(mt.at[0, t // SUBS, u_rows(t), :], u_ref(y, t), usem.at[y, t])

    def u_up(t):
        return remote(u_ref(y, t), uzs.at[t], usem.at[y, t], "row", up)

    def u_across(t):
        return remote(u_ref(y, t), uys.at[t], usem.at[y, t], "row", across)

    def u_other(t):
        return remote(u_ref(1 - y, t), uys.at[t], usem.at[1 - y, t], "row", across)

    def relay_u(t):
        @pl.when(z == 0)
        def _():
            u_load(t).wait()

        @pl.when(z > 0)
        def _():
            u_up(t).wait_recv()

        @pl.when(z < depth_z - 1)
        def _():
            u_up(t).start()

        u_across(t).start()

    def l_load(a):
        return pltpu.make_async_copy(mt.at[a, 0], lraw.at[k, a], lsem.at[k, a])

    def l_beyond(a):
        return remote(lraw.at[k, a], lxs.at[a], lsem.at[k, a], "col", beyond)

    def l_sibling(a):
        return remote(lraw.at[k, a], lks.at[a], lsem.at[k, a], "col", sibling)

    def l_other(a):
        return remote(lraw.at[1 - k, a], lks.at[a], lsem.at[1 - k, a], "col", sibling)

    def relay_l(a):
        @pl.when(x == 0)
        def _():
            l_load(a).wait()

        @pl.when(x > 0)
        def _():
            l_beyond(a).wait_recv()

        @pl.when(x < depth_x - 1)
        def _():
            l_beyond(a).start()

        l_sibling(a).start()

    def e_local():
        rows = pl.ds(pl.multiple_of(k * half, half), half)
        return pltpu.make_async_copy(lraw.at[1 - y, 0, rows, :], ebuf.at[y, k], esem.at[y, k])

    def e_up():
        return remote(ebuf.at[y, k], ezs.at[0], esem.at[y, k], "row", up)

    def e_across():
        return remote(ebuf.at[y, k], eys.at[0], esem.at[y, k], "row", across)

    def e_other():
        return remote(ebuf.at[1 - y, k], eys.at[0], esem.at[1 - y, k], "row", across)

    def e_sibling(lane):
        return remote(ebuf.at[lane, k], eks.at[lane], esem.at[lane, k], "col", sibling)

    def e_from_sibling(lane):
        return remote(ebuf.at[lane, 1 - k], eks.at[lane], esem.at[lane, 1 - k], "col", sibling)

    def relay_e():
        l_other(0).wait_recv()

        @pl.when(z == 0)
        def _():
            e_local().start()
            e_local().wait()

        @pl.when(z > 0)
        def _():
            e_up().wait_recv()

        @pl.when(z < depth_z - 1)
        def _():
            e_up().start()

        e_across().start()

    def unit_slice(ref, u):
        return ref.at[:, u // 2, pl.ds(pl.multiple_of((u % 2) * half, half), half), :]

    def unit_in(u):
        return pltpu.make_async_copy(unit_slice(mt, u), min_.at[u % 2], insem.at[u % 2])

    def unit_out(u):
        return pltpu.make_async_copy(mout.at[u % 2], unit_slice(out, u), outsem.at[u % 2])

    @pl.when(z == 0)
    def _():
        @pl.loop(0, n_sub)
        def _(t):
            u_load(t).start()

    @pl.when(x == 0)
    def _():
        for a in range(row_blocks):
            l_load(a).start()

    unit_in(0).start()
    unit_in(1).start()

    barrier = pltpu.get_barrier_semaphore()
    for d in range(1, grid_rows):
        pl.semaphore_signal(barrier, inc=1, device_id={"row": (me_r + d) % grid_rows},
                            device_id_type=MESH)
    for d in range(1, grid_cols):
        pl.semaphore_signal(barrier, inc=1, device_id={"col": (me_c + d) % grid_cols},
                            device_id_type=MESH)
    pl.semaphore_wait(barrier, grid_rows + grid_cols - 2)

    ahead = n_sub - n_unit
    l_steps = [a * ahead // row_blocks for a in range(row_blocks)]
    for t in range(ahead):
        relay_u(t)
        for a in range(row_blocks):
            if l_steps[a] == t:
                relay_l(a)
        if t == 5 * ahead // 12:
            relay_e()
        if t == 7 * ahead // 12:
            e_sibling(y).start()
            e_other().wait_recv()
            e_sibling(1 - y).start()
        if t < row_blocks:
            gcol[t] = jnp.broadcast_to(g[t:t + 1, :], (128, size)).T

    for lane in range(2):
        e_from_sibling(lane).wait_recv()
    zero = jnp.zeros((), bf16)
    upper = ebuf[0].reshape(size, size)
    lzb[...] = jnp.dot(ebuf[1].reshape(size, size), mult[0],
                       preferred_element_type=f32).astype(bf16)

    @pl.loop(1, row_blocks)
    def _(a):
        l_other(a).wait_recv()

    @pl.loop(0, row_blocks)
    def _(a):
        block_row = a * grid_rows + me_r
        first = jnp.dot(lraw[0, a], mult[0], preferred_element_type=f32).astype(bf16)
        first = jnp.where(block_row > 0, first, zero)
        lcat[a, :, :size] = first
        product = jnp.dot(first, ebuf[0].reshape(size, size), preferred_element_type=f32)
        column = (lraw[1, a].astype(f32) - product).astype(bf16)
        second = jnp.dot(column, mult[1], preferred_element_type=f32).astype(bf16)
        lcat[a, :, size:] = jnp.where(block_row > 1, second, zero)

    def compute(u):
        m, h, slot = u // 2, u % 2, u % 2
        block_col = m * grid_cols + me_c

        @pl.when(h == 0)
        def _():
            for s in range(SUBS):
                u_other(m * SUBS + s).wait_recv()
            first = jnp.where(block_col > 0, ubuf[0, m], zero)
            ucat[:size, :] = first
            product = jnp.dot(lzb[...], first, preferred_element_type=f32)
            second = (ubuf[1, m].astype(f32) - product).astype(bf16)
            ucat[size:, :] = jnp.where(block_col > 1, second, zero)
            csum[...] = jnp.zeros_like(csum)

        unit_in(u).wait()

        @pl.when(u >= 2)
        def _():
            unit_out(u - 2).wait()

        rows = pl.ds(pl.multiple_of(h * half, half), half)

        @pl.loop(0, row_blocks)
        def _(a):
            product = jnp.dot(lcat[a, rows, :], ucat[...], preferred_element_type=f32)
            result = min_[slot, a].astype(f32) - product
            mout[slot, a] = result.astype(bf16)
            weight = gcol[a, rows, :]
            weight = jnp.concatenate([weight] * (size // 128), axis=1)
            csum[...] += jnp.sum((weight * result).reshape(half // 8, 8, size), axis=0)

        for band in range(2):
            @pl.when(block_col == band)
            def _():
                @pl.loop(0, row_blocks)
                def _(a):
                    @pl.when(a * grid_rows + me_r > band)
                    def _():
                        mout[slot, a] = lcat[a, rows, band * size:(band + 1) * size]

        unit_out(u).start()

        @pl.when(u + 2 < n_unit)
        def _():
            unit_in(u + 2).start()

        @pl.when(h == 1)
        def _():
            crow[pl.ds(m, 1), :] = jnp.sum(csum[...], axis=0, keepdims=True)

    @pl.loop(ahead, n_sub + 2)
    def _(t):
        @pl.when(t < n_sub)
        def _():
            relay_u(t)

        @pl.when(t >= ahead + 2)
        def _():
            compute(t - ahead - 2)

    cbuf[me_r] = crow[...]
    group[...] = crow[...]

    def c_copy(d, slot, to):
        return pltpu.make_async_remote_copy(
            src_ref=crow, dst_ref=cbuf.at[slot], send_sem=csend.at[d], recv_sem=crecv.at[d],
            device_id={"row": to}, device_id_type=MESH)

    unit_out(n_unit - 2).wait()
    for d in range(1, grid_rows):
        c_copy(d - 1, me_r, (me_r + d) % grid_rows).start()

    @pl.loop(0, n_sub)
    def _(t):
        @pl.when(z < depth_z - 1)
        def _():
            u_up(t).wait_send()

        u_across(t).wait_send()

    for a in range(row_blocks):
        @pl.when(x < depth_x - 1)
        def _():
            l_beyond(a).wait_send()

        l_sibling(a).wait_send()

    @pl.when(z < depth_z - 1)
    def _():
        e_up().wait_send()

    e_across().wait_send()
    for lane in range(2):
        e_sibling(lane).wait_send()
    unit_out(n_unit - 1).wait()
    for d in range(1, grid_rows):
        origin = (me_r + grid_rows - d) % grid_rows
        c_copy(d - 1, origin, (me_r + d) % grid_rows).wait_recv()
        c_copy(d - 1, me_r, (me_r + d) % grid_rows).wait_send()
    summed = cbuf[0]
    for r in range(1, grid_rows):
        summed = summed + cbuf[r]
    total[...] = summed


def local(matrix, multiplier, checksum_weight):
    row_blocks, size, col_blocks, _ = matrix.shape
    grid_rows, grid_cols = lax.axis_size("row"), lax.axis_size("col")
    dims = (grid_rows, grid_cols, row_blocks, col_blocks, size)
    bf16, f32 = jnp.bfloat16, jnp.float32
    half, n_sub = size // 2, SUBS * col_blocks
    dma = pltpu.SemaphoreType.DMA
    vmem = pl.BlockSpec(memory_space=pltpu.VMEM)
    hbm = pl.BlockSpec(memory_space=pltpu.HBM)
    tiles = matrix.transpose(0, 2, 1, 3)
    out, group, total = pl.pallas_call(
        functools.partial(kernel, dims),
        out_shape=(
            jax.ShapeDtypeStruct(tiles.shape, bf16),
            jax.ShapeDtypeStruct((col_blocks, size), f32),
            jax.ShapeDtypeStruct((col_blocks, size), f32),
        ),
        in_specs=[hbm, vmem, vmem],
        out_specs=(hbm, vmem, vmem),
        scratch_shapes=[
            pltpu.VMEM((2, col_blocks, size, size), bf16),
            pltpu.VMEM((2, row_blocks, size, size), bf16),
            pltpu.VMEM((row_blocks, size, 2 * size), bf16),
            pltpu.VMEM((2, 2, half, size), bf16),
            pltpu.VMEM((size, size), bf16),
            pltpu.VMEM((2 * size, size), bf16),
            pltpu.VMEM((2, row_blocks, half, size), bf16),
            pltpu.VMEM((2, row_blocks, half, size), bf16),
            pltpu.VMEM((row_blocks, size, 128), f32),
            pltpu.VMEM((8, size), f32),
            pltpu.VMEM((col_blocks, size), f32),
            pltpu.VMEM((grid_rows, col_blocks, size), f32),
            dma((2, n_sub)), dma((n_sub,)), dma((n_sub,)),
            dma((2, row_blocks)), dma((row_blocks,)), dma((row_blocks,)),
            dma((2, 2)), dma((1,)), dma((1,)), dma((2,)),
            dma((2,)), dma((2,)),
            dma((grid_rows - 1,)), dma((grid_rows - 1,)),
        ],
        compiler_params=pltpu.CompilerParams(
            collective_id=0, has_side_effects=True, vmem_limit_bytes=60 * 1024 * 1024),
    )(tiles, multiplier, checksum_weight)
    return (out.transpose(0, 2, 1, 3), group.reshape(1, col_blocks, size), total)


def solution(mesh):
    in_specs = (P(None, "row", None, "col"), P(), P(None, "row"))
    out_specs = (P(None, "row", None, "col"), P("row", None, "col"), P(None, "col"))
    return jax.shard_map(local, mesh=mesh, in_specs=in_specs, out_specs=out_specs, check_vma=False)
```

```python
import functools

import jax
import jax.numpy as jnp
from jax import lax
from jax.experimental import pallas as pl
from jax.experimental.pallas import tpu as pltpu
from jax.sharding import PartitionSpec as P

SUBS = 4
MESH = pl.DeviceIdType.MESH


def kernel(dims, mt, mult, g, out, group, total, ubuf, lraw, lcat, ebuf, lzb, ucat, min_, mout,
           gcol, csum, crow, cbuf, usem, uzs, uys, lsem, lxs, lks, esem, ezs, eys, eks,
           insem, outsem, csend, crecv):
    grid_rows, grid_cols, row_blocks, col_blocks, size = dims
    f32, bf16 = jnp.float32, jnp.bfloat16
    sub, half = size // SUBS, size // 2
    me_r, me_c = lax.axis_index("row"), lax.axis_index("col")
    z, y, x, k = me_r // 2, me_r % 2, me_c // 2, me_c % 2
    depth_z, depth_x = grid_rows // 2, grid_cols // 2
    up, across = me_r + 2, me_r + 1 - 2 * y
    beyond, sibling = me_c + 2, me_c + 1 - 2 * k
    n_sub, n_unit = SUBS * col_blocks, 2 * col_blocks

    def remote(ref, send, recv, axis, to):
        return pltpu.make_async_remote_copy(
            src_ref=ref, dst_ref=ref, send_sem=send, recv_sem=recv,
            device_id={axis: to}, device_id_type=MESH)

    def u_rows(t):
        return pl.ds(pl.multiple_of((t % SUBS) * sub, sub), sub)

    def u_ref(band, t):
        return ubuf.at[band, t // SUBS, u_rows(t), :]

    def u_load(t):
        return pltpu.make_async_copy(mt.at[0, t // SUBS, u_rows(t), :], u_ref(y, t), usem.at[y, t])

    def u_up(t):
        return remote(u_ref(y, t), uzs.at[t], usem.at[y, t], "row", up)

    def u_across(t):
        return remote(u_ref(y, t), uys.at[t], usem.at[y, t], "row", across)

    def u_other(t):
        return remote(u_ref(1 - y, t), uys.at[t], usem.at[1 - y, t], "row", across)

    def relay_u(t):
        @pl.when(z == 0)
        def _():
            u_load(t).wait()

        @pl.when(z > 0)
        def _():
            u_up(t).wait_recv()

        @pl.when(z < depth_z - 1)
        def _():
            u_up(t).start()

        u_across(t).start()

    def l_load(a):
        return pltpu.make_async_copy(mt.at[a, 0], lraw.at[k, a], lsem.at[k, a])

    def l_beyond(a):
        return remote(lraw.at[k, a], lxs.at[a], lsem.at[k, a], "col", beyond)

    def l_sibling(a):
        return remote(lraw.at[k, a], lks.at[a], lsem.at[k, a], "col", sibling)

    def l_other(a):
        return remote(lraw.at[1 - k, a], lks.at[a], lsem.at[1 - k, a], "col", sibling)

    def relay_l(a):
        @pl.when(x == 0)
        def _():
            l_load(a).wait()

        @pl.when(x > 0)
        def _():
            l_beyond(a).wait_recv()

        @pl.when(x < depth_x - 1)
        def _():
            l_beyond(a).start()

        l_sibling(a).start()

    def e_local():
        rows = pl.ds(pl.multiple_of(k * half, half), half)
        return pltpu.make_async_copy(lraw.at[1 - y, 0, rows, :], ebuf.at[y, k], esem.at[y, k])

    def e_up():
        return remote(ebuf.at[y, k], ezs.at[0], esem.at[y, k], "row", up)

    def e_across():
        return remote(ebuf.at[y, k], eys.at[0], esem.at[y, k], "row", across)

    def e_other():
        return remote(ebuf.at[1 - y, k], eys.at[0], esem.at[1 - y, k], "row", across)

    def e_sibling(lane):
        return remote(ebuf.at[lane, k], eks.at[lane], esem.at[lane, k], "col", sibling)

    def e_from_sibling(lane):
        return remote(ebuf.at[lane, 1 - k], eks.at[lane], esem.at[lane, 1 - k], "col", sibling)

    def relay_e():
        l_other(0).wait_recv()

        @pl.when(z == 0)
        def _():
            e_local().start()
            e_local().wait()

        @pl.when(z > 0)
        def _():
            e_up().wait_recv()

        @pl.when(z < depth_z - 1)
        def _():
            e_up().start()

        e_across().start()

    def unit_slice(ref, u):
        return ref.at[:, u // 2, :, pl.ds(pl.multiple_of((u % 2) * half, half), half)]

    def unit_in(u):
        return pltpu.make_async_copy(unit_slice(mt, u), min_.at[u % 2], insem.at[u % 2])

    def unit_out(u):
        return pltpu.make_async_copy(mout.at[u % 2], unit_slice(out, u), outsem.at[u % 2])

    @pl.when(z == 0)
    def _():
        @pl.loop(0, n_sub)
        def _(t):
            u_load(t).start()

    @pl.when(x == 0)
    def _():
        for a in range(row_blocks):
            l_load(a).start()

    unit_in(0).start()
    unit_in(1).start()

    barrier = pltpu.get_barrier_semaphore()
    for d in range(1, grid_rows):
        pl.semaphore_signal(barrier, inc=1, device_id={"row": (me_r + d) % grid_rows},
                            device_id_type=MESH)
    for d in range(1, grid_cols):
        pl.semaphore_signal(barrier, inc=1, device_id={"col": (me_c + d) % grid_cols},
                            device_id_type=MESH)
    pl.semaphore_wait(barrier, grid_rows + grid_cols - 2)

    ahead = n_sub - n_unit
    l_steps = [a * ahead // row_blocks for a in range(row_blocks)]
    for t in range(ahead):
        relay_u(t)
        for a in range(row_blocks):
            if l_steps[a] == t:
                relay_l(a)
        if t == 5 * ahead // 12:
            relay_e()
        if t == 7 * ahead // 12:
            e_sibling(y).start()
            e_other().wait_recv()
            e_sibling(1 - y).start()
        if t < row_blocks:
            gcol[t] = jnp.broadcast_to(g[t:t + 1, :], (128, size)).T

    for lane in range(2):
        e_from_sibling(lane).wait_recv()
    zero = jnp.zeros((), bf16)
    upper = ebuf[0].reshape(size, size)
    lzb[...] = jnp.dot(ebuf[1].reshape(size, size), mult[0],
                       preferred_element_type=f32).astype(bf16)

    @pl.loop(1, row_blocks)
    def _(a):
        l_other(a).wait_recv()

    @pl.loop(0, row_blocks)
    def _(a):
        block_row = a * grid_rows + me_r
        first = jnp.dot(lraw[0, a], mult[0], preferred_element_type=f32).astype(bf16)
        first = jnp.where(block_row > 0, first, zero)
        lcat[a, :, :size] = first
        product = jnp.dot(first, ebuf[0].reshape(size, size), preferred_element_type=f32)
        column = (lraw[1, a].astype(f32) - product).astype(bf16)
        second = jnp.dot(column, mult[1], preferred_element_type=f32).astype(bf16)
        lcat[a, :, size:] = jnp.where(block_row > 1, second, zero)

    def compute(u):
        m, h, slot = u // 2, u % 2, u % 2
        block_col = m * grid_cols + me_c

        @pl.when(h == 0)
        def _():
            for s in range(SUBS):
                u_other(m * SUBS + s).wait_recv()
            first = jnp.where(block_col > 0, ubuf[0, m], zero)
            ucat[:size, :] = first
            product = jnp.dot(lzb[...], first, preferred_element_type=f32)
            second = (ubuf[1, m].astype(f32) - product).astype(bf16)
            ucat[size:, :] = jnp.where(block_col > 1, second, zero)

        csum[...] = jnp.zeros_like(csum)
        unit_in(u).wait()

        @pl.when(u >= 2)
        def _():
            unit_out(u - 2).wait()

        cols = pl.ds(pl.multiple_of(h * half, half), half)

        @pl.loop(0, row_blocks, unroll=True)
        def _(a):
            product = jnp.dot(lcat[a], ucat[:, cols], preferred_element_type=f32)
            result = min_[slot, a].astype(f32) - product
            mout[slot, a] = result.astype(bf16)
            weight = gcol[a]
            weight = jnp.concatenate([weight] * (half // 128), axis=1)
            csum[...] += jnp.sum((weight * result).reshape(size // 8, 8, half), axis=0)

        for band in range(2):
            @pl.when(block_col == band)
            def _():
                @pl.loop(0, row_blocks)
                def _(a):
                    @pl.when(a * grid_rows + me_r > band)
                    def _():
                        from_col = pl.multiple_of(band * size + h * half, half)
                        mout[slot, a] = lcat[a, :, pl.ds(from_col, half)]

        unit_out(u).start()

        @pl.when(u + 2 < n_unit)
        def _():
            unit_in(u + 2).start()

        crow[pl.ds(m, 1), cols] = jnp.sum(csum[...], axis=0, keepdims=True)

    @pl.loop(ahead, n_sub + 2)
    def _(t):
        @pl.when(t < n_sub)
        def _():
            relay_u(t)

        @pl.when(t >= ahead + 2)
        def _():
            compute(t - ahead - 2)

    cbuf[me_r] = crow[...]
    group[...] = crow[...]

    def c_copy(d, slot, to):
        return pltpu.make_async_remote_copy(
            src_ref=crow, dst_ref=cbuf.at[slot], send_sem=csend.at[d], recv_sem=crecv.at[d],
            device_id={"row": to}, device_id_type=MESH)

    unit_out(n_unit - 2).wait()
    for d in range(1, grid_rows):
        c_copy(d - 1, me_r, (me_r + d) % grid_rows).start()

    @pl.loop(0, n_sub)
    def _(t):
        @pl.when(z < depth_z - 1)
        def _():
            u_up(t).wait_send()

        u_across(t).wait_send()

    for a in range(row_blocks):
        @pl.when(x < depth_x - 1)
        def _():
            l_beyond(a).wait_send()

        l_sibling(a).wait_send()

    @pl.when(z < depth_z - 1)
    def _():
        e_up().wait_send()

    e_across().wait_send()
    for lane in range(2):
        e_sibling(lane).wait_send()
    unit_out(n_unit - 1).wait()
    for d in range(1, grid_rows):
        origin = (me_r + grid_rows - d) % grid_rows
        c_copy(d - 1, origin, (me_r + d) % grid_rows).wait_recv()
        c_copy(d - 1, me_r, (me_r + d) % grid_rows).wait_send()
    summed = cbuf[0]
    for r in range(1, grid_rows):
        summed = summed + cbuf[r]
    total[...] = summed


def local(matrix, multiplier, checksum_weight):
    row_blocks, size, col_blocks, _ = matrix.shape
    grid_rows, grid_cols = lax.axis_size("row"), lax.axis_size("col")
    dims = (grid_rows, grid_cols, row_blocks, col_blocks, size)
    bf16, f32 = jnp.bfloat16, jnp.float32
    half, n_sub = size // 2, SUBS * col_blocks
    dma = pltpu.SemaphoreType.DMA
    vmem = pl.BlockSpec(memory_space=pltpu.VMEM)
    hbm = pl.BlockSpec(memory_space=pltpu.HBM)
    tiles = matrix.transpose(0, 2, 1, 3)
    out, group, total = pl.pallas_call(
        functools.partial(kernel, dims),
        out_shape=(
            jax.ShapeDtypeStruct(tiles.shape, bf16),
            jax.ShapeDtypeStruct((col_blocks, size), f32),
            jax.ShapeDtypeStruct((col_blocks, size), f32),
        ),
        in_specs=[hbm, vmem, vmem],
        out_specs=(hbm, vmem, vmem),
        scratch_shapes=[
            pltpu.VMEM((2, col_blocks, size, size), bf16),
            pltpu.VMEM((2, row_blocks, size, size), bf16),
            pltpu.VMEM((row_blocks, size, 2 * size), bf16),
            pltpu.VMEM((2, 2, half, size), bf16),
            pltpu.VMEM((size, size), bf16),
            pltpu.VMEM((2 * size, size), bf16),
            pltpu.VMEM((2, row_blocks, size, half), bf16),
            pltpu.VMEM((2, row_blocks, size, half), bf16),
            pltpu.VMEM((row_blocks, size, 128), f32),
            pltpu.VMEM((8, half), f32),
            pltpu.VMEM((col_blocks, size), f32),
            pltpu.VMEM((grid_rows, col_blocks, size), f32),
            dma((2, n_sub)), dma((n_sub,)), dma((n_sub,)),
            dma((2, row_blocks)), dma((row_blocks,)), dma((row_blocks,)),
            dma((2, 2)), dma((1,)), dma((1,)), dma((2,)),
            dma((2,)), dma((2,)),
            dma((grid_rows - 1,)), dma((grid_rows - 1,)),
        ],
        compiler_params=pltpu.CompilerParams(
            collective_id=0, has_side_effects=True, vmem_limit_bytes=60 * 1024 * 1024),
    )(tiles, multiplier, checksum_weight)
    return (out.transpose(0, 2, 1, 3), group.reshape(1, col_blocks, size), total)


def solution(mesh):
    in_specs = (P(None, "row", None, "col"), P(), P(None, "row"))
    out_specs = (P(None, "row", None, "col"), P("row", None, "col"), P(None, "col"))
    return jax.shard_map(local, mesh=mesh, in_specs=in_specs, out_specs=out_specs, check_vma=False)
```
